32 devices in a mesh: bx: 8 (over z, x), bz: 4 (over y, core).
Axes of the slice: x: 2, y: 2, z: 4, core: 2. Of those that a mesh axis runs over, the one named last changes fastest.
Arguments:
- fields: bfloat16 [4, 32, 1024, 2048], P(None, 'bz', None, 'bx'), may hold values from -6 to 6
- breakpoints: int32 [8], replicated, may hold values from 0 to 255, as said below
- tf_color: float32 [8, 3], replicated, may hold values from 0.05 to 1
- tf_opacity: float32 [8], replicated, may hold values from 0.002 to 0.02
- depth_order: int32 [8, 4], replicated, may hold values from 0 to 3, each once within a row
- live_rows: int32 [8, 4, 2], P('bx', 'bz'), may hold values from 0 to 1024, as said below
Outputs:
- image: float32 [4, 1024, 2048], P(None, ('bx', 'bz'))
The draws below stay inside these ranges and needn't reach their ends.
Inputs may be any that keep to these rules, and one draw needn't show every extreme that they name: `breakpoints`: strictly increasing, first 0 and last 255. `live_rows`: for every brick the first row is below 512 and the end row above it; some brick starts at row 0 and some ends at row 1024.
All inputs are finite; a program needn't handle non-finite values.
Results may differ from the reference program's by a relative error of at most 0.0003.
Values may be sent and summed in bfloat16 or wider, within the bound.
A program may use at most 128 MiB of HBM per device.

```python
import math
import jax
import jax.numpy as jnp
from jax import lax

NF = 4
NBP = 8
BC = 256
Y = 1024
DZ = 8
IW = 2048
DEPTH = 32
N_BX = 8
N_BZ = 4


def draw_breakpoints(key, part):
    inner = jax.random.permutation(jax.random.fold_in(key, 11), 254)[:NBP - 2] + 1
    inner = jnp.sort(inner.astype(jnp.int32))
    return jnp.concatenate([jnp.zeros((1,), jnp.int32), inner, jnp.full((1,), 255, jnp.int32)]).astype(jnp.int32)


def draw_live_rows(key, part):
    first_key, second_key, third_key, fourth_key = jax.random.split(jax.random.fold_in(key, 23), 4)
    count = N_BX * N_BZ
    low = jax.random.randint(first_key, (N_BX, N_BZ), 0, Y // 2).astype(jnp.int32)
    high = (Y - jax.random.randint(second_key, (N_BX, N_BZ), 0, Y // 2)).astype(jnp.int32)
    flat = jnp.arange(count, dtype=jnp.int32).reshape(N_BX, N_BZ)
    chosen_low = jax.random.randint(third_key, (), 0, count).astype(jnp.int32)
    chosen_high = (chosen_low + 1 + jax.random.randint(fourth_key, (), 0, count - 1).astype(jnp.int32)) % count
    low = jnp.where(flat == chosen_low, 0, low)
    high = jnp.where(flat == chosen_high, Y, high)
    return jnp.stack([low, high], axis=-1).astype(jnp.int32)


def block_levels(rng, shape, cuts, smallest, high):
    loudness = 1.0
    for position, parts in cuts:
        steps = jax.random.uniform(jax.random.fold_in(jax.random.fold_in(rng, 6), position), (parts,), jnp.float32, smallest / len(cuts), high / len(cuts))
        loudness = loudness * jnp.repeat(jnp.exp(steps), shape[position] // parts).reshape((-1,) + (1,) * (len(shape) - 1 - position))
    return loudness


def scatter_about(rng, shape, deviation, limit, cuts=(), held_as=jnp.bfloat16):
    result = jax.random.normal(rng, shape, jnp.float32) * deviation
    if len(cuts) > 0:
        result = block_levels(rng, shape, cuts, -0.22, 0.18) * result
    return jnp.clip(result, min=-limit, max=limit).astype(held_as)


def setup_inputs(seed: int = 0) -> dict:
    key_of = jax.random.split(jax.random.key(seed), 7)
    return {
        "fields": scatter_about(key_of[0], (NF, DEPTH, Y, IW), 1.0, 6.0, ((1, 4), (3, 8))),
        "breakpoints": draw_breakpoints(jax.random.fold_in(key_of[6], 71), 0),
        "tf_color": jnp.clip(jax.random.uniform(key_of[2], (NBP, 3), jnp.float32, 0.05, 1.0), 0.05, 1.0),
        "tf_opacity": jnp.clip(jnp.exp(jax.random.uniform(key_of[3], (NBP,), jnp.float32, math.log(0.002), math.log(0.02))), 0.002, 0.02),
        "depth_order": jax.vmap(lambda own: jax.random.permutation(own, N_BZ))(jax.random.split(key_of[4], N_BX)).reshape((N_BX, N_BZ)).astype(jnp.int32),
        "live_rows": draw_live_rows(jax.random.fold_in(key_of[6], 71), 0),
    }


def classify(raw, breakpoints, tf_color, tf_opacity):
    level = 255.0 * jax.nn.sigmoid(raw[0])
    swirl = raw[1] * raw[1] + raw[2] * raw[2] + raw[3] * raw[3]
    marks = breakpoints.astype(jnp.float32)
    ramps = []
    for j in range(1, NBP):
        ramps.append(jnp.clip((level - marks[j - 1]) / (marks[j] - marks[j - 1]), 0.0, 1.0))

    def lookup(values):
        total = values[0] + jnp.zeros_like(level)
        for j in range(1, NBP):
            total = total + (values[j] - values[j - 1]) * ramps[j - 1]
        return total

    alpha = 1.0 - jnp.exp(-lookup(tf_opacity) * (0.25 + swirl))
    return jnp.stack([alpha * lookup(tf_color[:, 0]), alpha * lookup(tf_color[:, 1]), alpha * lookup(tf_color[:, 2]), alpha])


def reference(fields, breakpoints, tf_color, tf_opacity, depth_order, live_rows):
    reach = 3 * (DEPTH - 1) // 8 + 1
    rows = jnp.arange(Y, dtype=jnp.int32)
    partials = []
    for brick in range(N_BZ):
        def advance(k, acc):
            zglobal = (brick * DZ + k).astype(jnp.int32)
            raw = lax.dynamic_index_in_dim(fields, zglobal, 1, keepdims=False).astype(jnp.float32)
            sample = classify(raw, breakpoints, tf_color, tf_opacity)
            padded = jnp.pad(sample, ((0, 0), (0, 0), (reach, 0)))
            whole = (3 * zglobal) // 8
            frac = ((3 * zglobal) % 8).astype(jnp.float32) / 8.0
            near = lax.dynamic_slice_in_dim(padded, reach - whole, IW, 2)
            far = lax.dynamic_slice_in_dim(padded, reach - whole - 1, IW, 2)
            sheared = (1.0 - frac) * near + frac * far
            return acc + (1.0 - acc[3:4]) * sheared

        acc = lax.fori_loop(0, DZ, advance, jnp.zeros((4, Y, IW), jnp.float32))
        low = live_rows[:, brick, 0]
        high = live_rows[:, brick, 1]
        keep = ((rows[:, None] >= low[None, :]) & (rows[:, None] < high[None, :])).astype(jnp.float32)
        keep = jnp.repeat(keep, BC, axis=1)
        partials.append(acc * keep[None])
    stacked = jnp.stack(partials).reshape(N_BZ, 4, Y, N_BX, BC)
    slots = jnp.arange(N_BZ, dtype=jnp.int32)
    image = jnp.zeros((4, Y, N_BX, BC), jnp.float32)
    for k in range(N_BZ):
        pick = (depth_order[:, k][:, None] == slots[None, :]).astype(jnp.float32)
        chosen = jnp.zeros((4, Y, N_BX, BC), jnp.float32)
        for zslot in range(N_BZ):
            chosen = chosen + stacked[zslot] * pick[:, zslot][None, None, :, None]
        image = image + (1.0 - image[3:4]) * chosen
    return image.reshape(4, Y, IW)
```

```python
import functools

import jax
import jax.numpy as jnp
from jax import lax
from jax.experimental import pallas as pl
from jax.experimental.pallas import tpu as pltpu
from jax.sharding import PartitionSpec as P

LANES = 128
SUB = 16
LOG2E = 1.4426950408889634
CODE = 65535.0


def encode(value):
    root = jnp.sqrt(jnp.sqrt(jnp.maximum(value, 0.0)))
    return jnp.round(root * CODE - 32768.0).astype(jnp.int32).astype(jnp.int16)


def decode(code):
    root = (code.astype(jnp.int32).astype(jnp.float32) + 32768.0) * (1.0 / CODE)
    square = root * root
    return square * square


def halo_pitch(reach):
    pitch = 16
    while pitch < reach:
        pitch *= 2
    return pitch


def pack_kernel(pitch, src_ref, dst_ref):
    slices = src_ref.shape[1]
    per = LANES // pitch
    lane = lax.broadcasted_iota(jnp.int32, (src_ref.shape[2], LANES), 1)
    for f in range(src_ref.shape[0]):
        for v in range(dst_ref.shape[2] // LANES):
            total = jnp.zeros((src_ref.shape[2], LANES), jnp.float32)
            for s in range(per):
                k = v * per + s
                if k < slices:
                    x = src_ref[f, k].astype(jnp.float32)
                    x = pltpu.roll(x, (s + 1) * pitch % LANES, 1)
                    slot = (lane >= s * pitch) & (lane < (s + 1) * pitch)
                    total = jnp.where(slot, x, total)
            dst_ref[f, :, v * LANES : (v + 1) * LANES] = total.astype(jnp.bfloat16)


def pack_halo(fields, pitch):
    nf, slices, height, width = fields.shape
    rows = 128
    lanes = -(-slices * pitch // LANES) * LANES
    return pl.pallas_call(
        functools.partial(pack_kernel, pitch),
        grid=(height // rows,),
        in_specs=[pl.BlockSpec((nf, slices, rows, LANES), lambda r: (0, 0, r, width // LANES - 1))],
        out_specs=pl.BlockSpec((nf, rows, lanes), lambda r: (0, r, 0)),
        out_shape=jax.ShapeDtypeStruct((nf, height, lanes), jnp.bfloat16),
        name="pack_halo",
    )(fields)


def build_tables(marks_ref, color_ref, opacity_ref, tab_ref):
    nbp = marks_ref.shape[0]
    lane = lax.broadcasted_iota(jnp.int32, (SUB, LANES), 1)

    def spread(value):
        total = jnp.zeros((SUB, LANES), jnp.float32)
        for j in range(nbp - 1):
            total = jnp.where(lane == j, value(j), total)
        return total

    mark = lambda j: marks_ref[j].astype(jnp.float32)
    start = spread(mark)
    step = jnp.where(lane < nbp - 1, spread(lambda j: mark(j + 1)) - start, 1.0)
    for q in range(4):
        value = (lambda j: color_ref[3 * j + q]) if q < 3 else (lambda j: opacity_ref[j])
        first = spread(value)
        slope = (spread(lambda j: value(j + 1)) - first) / step
        base = first - slope * start
        scale = 1.0 if q < 3 else -LOG2E
        tab_ref[2 * q] = base * scale
        tab_ref[2 * q + 1] = slope * scale


def make_classify(marks_ref, tab_ref):
    nbp = marks_ref.shape[0]
    marks = [marks_ref[j].astype(jnp.float32) for j in range(nbp)]
    rows_of = lambda q: tab_ref[q]

    def look(q, seg):
        return jnp.take_along_axis(rows_of(q), seg, axis=1, mode="promise_in_bounds")

    def classify(raw):
        x0, x1, x2, x3 = [r.astype(jnp.float32) for r in raw]
        level = 127.5 * jnp.tanh(0.5 * x0) + 127.5
        swirl = x1 * x1 + x2 * x2 + x3 * x3
        seg = jnp.zeros(level.shape, jnp.int32)
        for j in range(1, nbp - 1):
            seg = jnp.where(level >= marks[j], j, seg)
        rate = look(6, seg) + look(7, seg) * level
        alpha = 1.0 - jnp.exp2(rate * (0.25 + swirl))
        return [alpha * (look(2 * q, seg) + look(2 * q + 1, seg) * level) for q in range(3)] + [alpha]

    return classify


def turn(parts, shift, lane):
    rolled = [pltpu.roll(p, shift, 1) for p in parts]
    return [jnp.where(lane < shift, rolled[i - 1], rolled[i]) for i in range(len(parts))]


def turn_back(parts, lane):
    rolled = [pltpu.roll(p, LANES - 1, 1) for p in parts]
    n = len(parts)
    return [jnp.where(lane == LANES - 1, rolled[(i + 1) % n], rolled[i]) for i in range(n)]


def volume_kernel(pitch, marks_ref, color_ref, opacity_ref, live_ref, fields_ref, halo_ref, out_ref, tab_ref):
    nf, slices, rows, width = fields_ref.shape
    nv = width // LANES
    per = LANES // pitch
    step = pl.program_id(0)

    @pl.when(step == 0)
    def _():
        build_tables(marks_ref, color_ref, opacity_ref, tab_ref)

    low = live_ref[0]
    high = live_ref[1]
    row0 = step * rows
    alive = (row0 < high) & (row0 + rows > low)
    edge = jnp.where(lax.axis_index("bx") > 0, 1.0, 0.0).astype(jnp.float32)
    base = 3 * (lax.axis_index("bz") * slices) // 8

    @pl.when(jnp.logical_not(alive))
    def _():
        out_ref[...] = jnp.full(out_ref.shape, -32768, jnp.int16)

    @pl.when(alive)
    def _():
        lane = lax.broadcasted_iota(jnp.int32, (SUB, LANES), 1)
        sub = lax.broadcasted_iota(jnp.int32, (SUB, LANES), 0)
        classify = make_classify(marks_ref, tab_ref)

        def group(g, carry):
            at = pl.ds(pl.multiple_of(g * SUB, SUB), SUB)
            halo = []
            for v in range(halo_ref.shape[2] // LANES):
                s = classify([halo_ref[f, at, v * LANES : (v + 1) * LANES] for f in range(nf)])
                halo.append([c * edge for c in s])
            color = [[jnp.zeros((SUB, LANES), jnp.float32) for _ in range(nv)] for _ in range(3)]
            clear = [jnp.ones((SUB, LANES), jnp.float32) for _ in range(nv)]
            for k in range(slices):
                whole = 3 * k // 8
                frac = (3 * k % 8) / 8.0
                if k > 0 and whole > 3 * (k - 1) // 8:
                    color = [turn_back(c, lane) for c in color]
                    clear = turn_back(clear, lane)
                a = base + whole
                by_part = [
                    classify([fields_ref[f, k, at, v * LANES : (v + 1) * LANES] for f in range(nf)])
                    for v in range(nv)
                ]
                sheared = []
                for q in range(4):
                    parts = [by_part[v][q] for v in range(nv)]
                    held = halo[k // per][q]
                    to = (LANES - (k % per + 1) * pitch) % LANES
                    near_halo = pltpu.roll(held, to, 1) if to else held
                    parts[-1] = jnp.where(lane >= LANES - a, near_halo, parts[-1])
                    if frac > 0:
                        far = turn(parts, 1, lane)
                        far_halo = pltpu.roll(held, to + 1, 1)
                        spot = jnp.where(a == 0, 0, LANES - a)
                        first = (lane == spot) & (a == 0)
                        last = (lane == spot) & (a > 0)
                        far[0] = jnp.where(first, far_halo, far[0])
                        far[-1] = jnp.where(last, far_halo, far[-1])
                        parts = [p + frac * (r - p) for p, r in zip(parts, far)]
                    sheared.append(parts)
                for q in range(3):
                    color[q] = [c + t * s for c, t, s in zip(color[q], clear, sheared[q])]
                clear = [t - t * s for t, s in zip(clear, sheared[3])]
            end = base + 3 * (slices - 1) // 8
            row = row0 + g * SUB + sub
            keep = (row >= low) & (row < high)
            for q in range(4):
                parts = color[q] if q < 3 else [1.0 - t for t in clear]
                parts = turn(parts, end, lane)
                for v in range(nv):
                    out_ref[0, q, 0, at, v * LANES : (v + 1) * LANES] = encode(jnp.where(keep, parts[v], 0.0))
            return carry

        lax.fori_loop(0, rows // SUB, group, 0)


def volume(fields, halo, breakpoints, tf_color, tf_opacity, live, pitch, count_x, count_z):
    nf, slices, height, width = fields.shape
    assert slices % 8 == 0
    owned = height // (count_x * count_z)
    smem = pl.BlockSpec(memory_space=pltpu.SMEM)
    return pl.pallas_call(
        functools.partial(volume_kernel, pitch),
        grid=(count_x * count_z,),
        in_specs=[
            smem,
            smem,
            smem,
            smem,
            pl.BlockSpec((nf, slices, owned, width), lambda r: (0, 0, r, 0)),
            pl.BlockSpec((nf, owned, halo.shape[2]), lambda r: (0, r, 0)),
        ],
        out_specs=pl.BlockSpec((1, 4, 1, owned, width), lambda r: (r % count_z, 0, r // count_z, 0, 0)),
        out_shape=jax.ShapeDtypeStruct((count_z, 4, count_x, owned, width), jnp.int16),
        scratch_shapes=[pltpu.VMEM((8, SUB, LANES), jnp.float32)],
        name="volume",
    )(breakpoints, tf_color.reshape(-1), tf_opacity, live, fields, halo)


def merge_kernel(order_ref, src_ref, dst_ref):
    depth = src_ref.shape[0]
    column = lax.axis_index("bx")
    rows = src_ref.shape[3]
    for g in range(0, rows, SUB):
        at = slice(g, g + SUB)
        total = None
        for k in range(depth):
            d = order_ref[column * depth + k]
            part = [decode(src_ref[d, q, 0, at]) for q in range(4)]
            if total is None:
                total = part
            else:
                clear = 1.0 - total[3]
                total = [t + clear * p for t, p in zip(total, part)]
        for q in range(4):
            dst_ref[0, q, at] = encode(total[q])


def merge(arrived, order):
    depth, _, count_x, owned, width = arrived.shape
    return pl.pallas_call(
        merge_kernel,
        grid=(count_x,),
        in_specs=[
            pl.BlockSpec(memory_space=pltpu.SMEM),
            pl.BlockSpec((depth, 4, 1, owned, width), lambda i: (0, 0, i, 0, 0)),
        ],
        out_specs=pl.BlockSpec((1, 4, owned, width), lambda i: (i, 0, 0, 0)),
        out_shape=jax.ShapeDtypeStruct((count_x, 4, owned, width), jnp.int16),
        name="merge",
    )(order.reshape(-1), arrived)


def open_kernel(src_ref, dst_ref):
    dst_ref[...] = decode(src_ref[0])


def open_image(moved):
    count_x, _, owned, width = moved.shape
    return pl.pallas_call(
        open_kernel,
        grid=(count_x,),
        in_specs=[pl.BlockSpec((1, 4, owned, width), lambda i: (i, 0, 0, 0))],
        out_specs=pl.BlockSpec((4, owned, width), lambda i: (0, 0, i)),
        out_shape=jax.ShapeDtypeStruct((4, owned, count_x * width), jnp.float32),
        name="open_image",
    )(moved)


def per_device(fields, breakpoints, tf_color, tf_opacity, depth_order, live_rows):
    slices = fields.shape[1]
    count_x = lax.axis_size("bx")
    count_z = lax.axis_size("bz")
    reach = 3 * (slices * count_z - 1) // 8 + 1
    pitch = halo_pitch(reach)
    rim = pack_halo(fields, pitch)
    halo = lax.ppermute(rim, "bx", [(i, i + 1) for i in range(count_x - 1)])
    live = live_rows.reshape(2)
    partial = volume(fields, halo, breakpoints, tf_color, tf_opacity, live, pitch, count_x, count_z)
    arrived = lax.all_to_all(partial, "bz", split_axis=0, concat_axis=0, tiled=True)
    merged = merge(arrived, depth_order)
    moved = lax.all_to_all(merged, "bx", split_axis=0, concat_axis=0, tiled=True)
    return open_image(moved)


def solution(mesh):
    return jax.shard_map(
        per_device,
        mesh=mesh,
        in_specs=(P(None, "bz", None, "bx"), P(), P(), P(), P(), P("bx", "bz", None)),
        out_specs=P(None, ("bx", "bz"), None),
        check_vma=False,
    )
```

```python
import functools

import jax
import jax.numpy as jnp
from jax import lax
from jax.experimental import pallas as pl
from jax.experimental.pallas import tpu as pltpu
from jax.sharding import PartitionSpec as P

LANES = 128
SUB = 16
LOG2E = 1.4426950408889634
CODE = 65535.0


def encode(value):
    root = jnp.sqrt(jnp.sqrt(jnp.maximum(value, 0.0)))
    return jnp.round(root * CODE - 32768.0).astype(jnp.int32).astype(jnp.int16)


def decode(code):
    root = (code.astype(jnp.int32).astype(jnp.float32) + 32768.0) * (1.0 / CODE)
    square = root * root
    return square * square


def halo_pitch(reach):
    pitch = 16
    while pitch < reach:
        pitch *= 2
    return pitch


def pack_kernel(pitch, src_ref, dst_ref):
    slices = src_ref.shape[1]
    per = LANES // pitch
    lane = lax.broadcasted_iota(jnp.int32, (src_ref.shape[2], LANES), 1)
    for f in range(src_ref.shape[0]):
        for v in range(dst_ref.shape[2] // LANES):
            total = jnp.zeros((src_ref.shape[2], LANES), jnp.float32)
            for s in range(per):
                k = v * per + s
                if k < slices:
                    x = src_ref[f, k].astype(jnp.float32)
                    x = pltpu.roll(x, (s + 1) * pitch % LANES, 1)
                    slot = (lane >= s * pitch) & (lane < (s + 1) * pitch)
                    total = jnp.where(slot, x, total)
            dst_ref[f, :, v * LANES : (v + 1) * LANES] = total.astype(jnp.bfloat16)


def pack_halo(fields, pitch):
    nf, slices, height, width = fields.shape
    rows = 128
    lanes = -(-slices * pitch // LANES) * LANES
    return pl.pallas_call(
        functools.partial(pack_kernel, pitch),
        grid=(height // rows,),
        in_specs=[pl.BlockSpec((nf, slices, rows, LANES), lambda r: (0, 0, r, width // LANES - 1))],
        out_specs=pl.BlockSpec((nf, rows, lanes), lambda r: (0, r, 0)),
        out_shape=jax.ShapeDtypeStruct((nf, height, lanes), jnp.bfloat16),
        name="pack_halo",
    )(fields)


def build_tables(marks_ref, color_ref, opacity_ref, tab_ref):
    nbp = marks_ref.shape[0]
    lane = lax.broadcasted_iota(jnp.int32, (8, LANES), 0)

    def spread(value):
        total = jnp.zeros((8, LANES), jnp.float32)
        for j in range(nbp - 1):
            total = jnp.where(lane == j, value(j), total)
        return total

    mark = lambda j: marks_ref[j].astype(jnp.float32)
    start = spread(mark)
    step = jnp.where(lane < nbp - 1, spread(lambda j: mark(j + 1)) - start, 1.0)
    for q in range(4):
        value = (lambda j: color_ref[3 * j + q]) if q < 3 else (lambda j: opacity_ref[j])
        first = spread(value)
        slope = (spread(lambda j: value(j + 1)) - first) / step
        base = first - slope * start
        scale = 1.0 if q < 3 else -LOG2E
        tab_ref[2 * q] = base * scale
        tab_ref[2 * q + 1] = slope * scale


def make_classify(marks_ref, tab_ref):
    nbp = marks_ref.shape[0]
    marks = [marks_ref[j].astype(jnp.float32) for j in range(nbp)]
    rows_of = lambda q: tab_ref[q]

    def look(q, seg):
        return jnp.concatenate([jnp.take_along_axis(rows_of(q), seg[i : i + 8], axis=0, mode="promise_in_bounds") for i in range(0, SUB, 8)], axis=0)

    def classify(raw):
        x0, x1, x2, x3 = [r.astype(jnp.float32) for r in raw]
        level = 127.5 * jnp.tanh(0.5 * x0) + 127.5
        swirl = x1 * x1 + x2 * x2 + x3 * x3
        seg = jnp.zeros(level.shape, jnp.int32)
        for j in range(1, nbp - 1):
            seg = jnp.where(level >= marks[j], j, seg)
        rate = look(6, seg) + look(7, seg) * level
        alpha = 1.0 - jnp.exp2(rate * (0.25 + swirl))
        return [alpha * (look(2 * q, seg) + look(2 * q + 1, seg) * level) for q in range(3)] + [alpha]

    return classify


def turn(parts, shift, lane):
    rolled = [pltpu.roll(p, shift, 1) for p in parts]
    return [jnp.where(lane < shift, rolled[i - 1], rolled[i]) for i in range(len(parts))]


def turn_back(parts, lane):
    rolled = [pltpu.roll(p, LANES - 1, 1) for p in parts]
    n = len(parts)
    return [jnp.where(lane == LANES - 1, rolled[(i + 1) % n], rolled[i]) for i in range(n)]


def volume_kernel(pitch, marks_ref, color_ref, opacity_ref, live_ref, fields_ref, halo_ref, out_ref, tab_ref):
    nf, slices, rows, width = fields_ref.shape
    nv = width // LANES
    per = LANES // pitch
    step = pl.program_id(0)

    @pl.when(step == 0)
    def _():
        build_tables(marks_ref, color_ref, opacity_ref, tab_ref)

    low = live_ref[0]
    high = live_ref[1]
    row0 = step * rows
    alive = (row0 < high) & (row0 + rows > low)
    edge = jnp.where(lax.axis_index("bx") > 0, 1.0, 0.0).astype(jnp.float32)
    base = 3 * (lax.axis_index("bz") * slices) // 8

    @pl.when(jnp.logical_not(alive))
    def _():
        out_ref[...] = jnp.full(out_ref.shape, -32768, jnp.int16)

    @pl.when(alive)
    def _():
        lane = lax.broadcasted_iota(jnp.int32, (SUB, LANES), 1)
        sub = lax.broadcasted_iota(jnp.int32, (SUB, LANES), 0)
        classify = make_classify(marks_ref, tab_ref)

        def group(g, carry):
            at = pl.ds(pl.multiple_of(g * SUB, SUB), SUB)
            halo = []
            for v in range(halo_ref.shape[2] // LANES):
                s = classify([halo_ref[f, at, v * LANES : (v + 1) * LANES] for f in range(nf)])
                halo.append([c * edge for c in s])
            color = [[jnp.zeros((SUB, LANES), jnp.float32) for _ in range(nv)] for _ in range(3)]
            clear = [jnp.ones((SUB, LANES), jnp.float32) for _ in range(nv)]
            for k in range(slices):
                whole = 3 * k // 8
                frac = (3 * k % 8) / 8.0
                if k > 0 and whole > 3 * (k - 1) // 8:
                    color = [turn_back(c, lane) for c in color]
                    clear = turn_back(clear, lane)
                a = base + whole
                by_part = [
                    classify([fields_ref[f, k, at, v * LANES : (v + 1) * LANES] for f in range(nf)])
                    for v in range(nv)
                ]
                sheared = []
                for q in range(4):
                    parts = [by_part[v][q] for v in range(nv)]
                    held = halo[k // per][q]
                    to = (LANES - (k % per + 1) * pitch) % LANES
                    held = pltpu.roll(held, to, 1) if to else held
                    own = parts[-1]
                    parts[-1] = jnp.where(lane >= LANES - a, held, own)
                    if frac > 0:
                        far = parts[:-1] + [jnp.where(lane >= LANES - 1 - a, held, own)]
                        far = turn(far, 1, lane)
                        parts = [p + frac * (r - p) for p, r in zip(parts, far)]
                    sheared.append(parts)
                for q in range(3):
                    color[q] = [c + t * s for c, t, s in zip(color[q], clear, sheared[q])]
                clear = [t - t * s for t, s in zip(clear, sheared[3])]
            end = base + 3 * (slices - 1) // 8
            row = row0 + g * SUB + sub
            keep = (row >= low) & (row < high)
            for q in range(4):
                parts = color[q] if q < 3 else [1.0 - t for t in clear]
                parts = turn(parts, end, lane)
                for v in range(nv):
                    out_ref[0, q, 0, at, v * LANES : (v + 1) * LANES] = encode(jnp.where(keep, parts[v], 0.0))
            return carry

        lax.fori_loop(0, rows // SUB, group, 0)


def volume(fields, halo, breakpoints, tf_color, tf_opacity, live, pitch, count_x, count_z):
    nf, slices, height, width = fields.shape
    assert slices % 8 == 0
    owned = height // (count_x * count_z)
    smem = pl.BlockSpec(memory_space=pltpu.SMEM)
    return pl.pallas_call(
        functools.partial(volume_kernel, pitch),
        grid=(count_x * count_z,),
        in_specs=[
            smem,
            smem,
            smem,
            smem,
            pl.BlockSpec((nf, slices, owned, width), lambda r: (0, 0, r, 0)),
            pl.BlockSpec((nf, owned, halo.shape[2]), lambda r: (0, r, 0)),
        ],
        out_specs=pl.BlockSpec((1, 4, 1, owned, width), lambda r: (r % count_z, 0, r // count_z, 0, 0)),
        out_shape=jax.ShapeDtypeStruct((count_z, 4, count_x, owned, width), jnp.int16),
        scratch_shapes=[pltpu.VMEM((8, 8, LANES), jnp.float32)],
        name="volume",
    )(breakpoints, tf_color.reshape(-1), tf_opacity, live, fields, halo)


def merge_kernel(order_ref, src_ref, dst_ref):
    depth = src_ref.shape[0]
    column = lax.axis_index("bx")
    rows = src_ref.shape[3]
    for g in range(0, rows, SUB):
        at = slice(g, g + SUB)
        total = None
        for k in range(depth):
            d = order_ref[column * depth + k]
            part = [decode(src_ref[d, q, 0, at]) for q in range(4)]
            if total is None:
                total = part
            else:
                clear = 1.0 - total[3]
                total = [t + clear * p for t, p in zip(total, part)]
        for q in range(4):
            dst_ref[0, q, at] = encode(total[q])


def merge(arrived, order):
    depth, _, count_x, owned, width = arrived.shape
    return pl.pallas_call(
        merge_kernel,
        grid=(count_x,),
        in_specs=[
            pl.BlockSpec(memory_space=pltpu.SMEM),
            pl.BlockSpec((depth, 4, 1, owned, width), lambda i: (0, 0, i, 0, 0)),
        ],
        out_specs=pl.BlockSpec((1, 4, owned, width), lambda i: (i, 0, 0, 0)),
        out_shape=jax.ShapeDtypeStruct((count_x, 4, owned, width), jnp.int16),
        name="merge",
    )(order.reshape(-1), arrived)


def open_kernel(src_ref, dst_ref):
    dst_ref[...] = decode(src_ref[0])


def open_image(moved):
    count_x, _, owned, width = moved.shape
    return pl.pallas_call(
        open_kernel,
        grid=(count_x,),
        in_specs=[pl.BlockSpec((1, 4, owned, width), lambda i: (i, 0, 0, 0))],
        out_specs=pl.BlockSpec((4, owned, width), lambda i: (0, 0, i)),
        out_shape=jax.ShapeDtypeStruct((4, owned, count_x * width), jnp.float32),
        name="open_image",
    )(moved)


def per_device(fields, breakpoints, tf_color, tf_opacity, depth_order, live_rows):
    slices = fields.shape[1]
    count_x = lax.axis_size("bx")
    count_z = lax.axis_size("bz")
    reach = 3 * (slices * count_z - 1) // 8 + 1
    pitch = halo_pitch(reach)
    rim = pack_halo(fields, pitch)
    halo = lax.ppermute(rim, "bx", [(i, i + 1) for i in range(count_x - 1)])
    live = live_rows.reshape(2)
    partial = volume(fields, halo, breakpoints, tf_color, tf_opacity, live, pitch, count_x, count_z)
    arrived = lax.all_to_all(partial, "bz", split_axis=0, concat_axis=0, tiled=True)
    merged = merge(arrived, depth_order)
    moved = lax.all_to_all(merged, "bx", split_axis=0, concat_axis=0, tiled=True)
    return open_image(moved)


def solution(mesh):
    return jax.shard_map(
        per_device,
        mesh=mesh,
        in_specs=(P(None, "bz", None, "bx"), P(), P(), P(), P(), P("bx", "bz", None)),
        out_specs=P(None, ("bx", "bz"), None),
        check_vma=False,
    )
```

```python
import functools
import math

import jax
import jax.numpy as jnp
from jax import lax
from jax.experimental import pallas as pl
from jax.experimental.pallas import tpu as pltpu
from jax.sharding import PartitionSpec as P


LANES = 128
SUB = 16
LOG2E = 1.4426950408889634
CODE = 65535.0
CHUNKS = 2


def encode(value):
    root = jnp.sqrt(jnp.sqrt(jnp.maximum(value, 0.0)))
    return jnp.round(root * CODE - 32768.0).astype(jnp.int32).astype(jnp.int16)


def decode(code):
    root = (code.astype(jnp.int32).astype(jnp.float32) + 32768.0) * (1.0 / CODE)
    square = root * root
    return square * square


def halo_pitch(reach):
    pitch = 16
    while pitch < reach:
        pitch *= 2
    return pitch


def pack_kernel(pitch, src_ref, dst_ref):
    slices = src_ref.shape[1]
    per = LANES // pitch
    lane = lax.broadcasted_iota(jnp.int32, (src_ref.shape[2], LANES), 1)
    for f in range(src_ref.shape[0]):
        for v in range(dst_ref.shape[2] // LANES):
            total = jnp.zeros((src_ref.shape[2], LANES), jnp.float32)
            for s in range(per):
                k = v * per + s
                if k < slices:
                    x = src_ref[f, k].astype(jnp.float32)
                    x = pltpu.roll(x, (s + 1) * pitch % LANES, 1)
                    slot = (lane >= s * pitch) & (lane < (s + 1) * pitch)
                    total = jnp.where(slot, x, total)
            dst_ref[f, :, v * LANES : (v + 1) * LANES] = total.astype(jnp.bfloat16)


def pack_halo(fields, pitch, chunk, chunks):
    nf, slices, height, width = fields.shape
    rows = 64
    lanes = -(-slices * pitch // LANES) * LANES
    steps = height // chunks // rows
    return pl.pallas_call(
        functools.partial(pack_kernel, pitch),
        grid=(steps,),
        in_specs=[
            pl.BlockSpec((nf, slices, rows, LANES), lambda r: (0, 0, r + chunk * steps, width // LANES - 1))
        ],
        out_specs=pl.BlockSpec((nf, rows, lanes), lambda r: (0, r, 0)),
        out_shape=jax.ShapeDtypeStruct((nf, height // chunks, lanes), jnp.bfloat16),
        cost_estimate=pl.CostEstimate(
            flops=height // chunks * LANES * nf * slices * 4,
            bytes_accessed=height // chunks * LANES * nf * slices * 2,
            transcendentals=0,
        ),
        name="pack_halo",
    )(fields)


def build_tables(marks_ref, color_ref, opacity_ref, tab_ref):
    nbp = marks_ref.shape[0]
    lane = lax.broadcasted_iota(jnp.int32, (8, LANES), 0)

    def spread(value):
        total = jnp.zeros((8, LANES), jnp.float32)
        for j in range(nbp - 1):
            total = jnp.where(lane == j, value(j), total)
        return total

    mark = lambda j: marks_ref[j].astype(jnp.float32)
    start = spread(mark)
    step = jnp.where(lane < nbp - 1, spread(lambda j: mark(j + 1)) - start, 1.0)
    for q in range(4):
        value = (lambda j: color_ref[3 * j + q]) if q < 3 else (lambda j: opacity_ref[j])
        first = spread(value)
        slope = (spread(lambda j: value(j + 1)) - first) / step
        base = first - slope * start
        scale = 1.0 if q < 3 else -LOG2E
        tab_ref[2 * q] = base * scale
        tab_ref[2 * q + 1] = slope * scale


def make_classify(marks_ref, tab_ref):
    nbp = marks_ref.shape[0]
    marks = [marks_ref[j].astype(jnp.float32) for j in range(nbp)]
    rows_of = lambda q: tab_ref[q]

    def look(q, seg):
        return jnp.concatenate([jnp.take_along_axis(rows_of(q), seg[i : i + 8], axis=0, mode="promise_in_bounds") for i in range(0, SUB, 8)], axis=0)

    def classify(raw):
        x0, x1, x2, x3 = [r.astype(jnp.float32) for r in raw]
        level = 127.5 * jnp.tanh(0.5 * x0) + 127.5
        swirl = x1 * x1 + x2 * x2 + x3 * x3
        seg = jnp.zeros(level.shape, jnp.int32)
        for j in range(1, nbp - 1):
            seg = jnp.where(level >= marks[j], j, seg)
        rate = look(6, seg) + look(7, seg) * level
        alpha = 1.0 - jnp.exp2(rate * (0.25 + swirl))
        return [alpha * (look(2 * q, seg) + look(2 * q + 1, seg) * level) for q in range(3)] + [alpha]

    return classify


def turn(parts, shift, lane):
    rolled = [pltpu.roll(p, shift, 1) for p in parts]
    return [jnp.where(lane < shift, rolled[i - 1], rolled[i]) for i in range(len(parts))]


def turn_back(parts, lane):
    rolled = [pltpu.roll(p, LANES - 1, 1) for p in parts]
    n = len(parts)
    return [jnp.where(lane == LANES - 1, rolled[(i + 1) % n], rolled[i]) for i in range(n)]


def volume_kernel(pitch, first_step, marks_ref, color_ref, opacity_ref, live_ref, fields_ref, halo_ref, *rest):
    out_ref, tab_ref = rest[-2:]
    nf, slices, rows, width = fields_ref.shape
    nv = width // LANES
    per = LANES // pitch
    step = pl.program_id(0)

    @pl.when(step == 0)
    def _():
        build_tables(marks_ref, color_ref, opacity_ref, tab_ref)

    low = live_ref[0]
    high = live_ref[1]
    row0 = (step + first_step) * rows
    alive = (row0 < high) & (row0 + rows > low)
    edge = jnp.where(lax.axis_index("bx") > 0, 1.0, 0.0).astype(jnp.float32)
    base = 3 * (lax.axis_index("bz") * slices) // 8

    @pl.when(jnp.logical_not(alive))
    def _():
        out_ref[...] = jnp.full(out_ref.shape, -32768, jnp.int16)

    @pl.when(alive)
    def _():
        lane = lax.broadcasted_iota(jnp.int32, (SUB, LANES), 1)
        sub = lax.broadcasted_iota(jnp.int32, (SUB, LANES), 0)
        classify = make_classify(marks_ref, tab_ref)

        def group(g, carry):
            at = pl.ds(pl.multiple_of(g * SUB, SUB), SUB)
            halo = []
            for v in range(halo_ref.shape[2] // LANES):
                s = classify([halo_ref[f, at, v * LANES : (v + 1) * LANES] for f in range(nf)])
                halo.append([c * edge for c in s])
            color = [[jnp.zeros((SUB, LANES), jnp.float32) for _ in range(nv)] for _ in range(3)]
            clear = [jnp.ones((SUB, LANES), jnp.float32) for _ in range(nv)]
            for k in range(slices):
                whole = 3 * k // 8
                frac = (3 * k % 8) / 8.0
                if k > 0 and whole > 3 * (k - 1) // 8:
                    color = [turn_back(c, lane) for c in color]
                    clear = turn_back(clear, lane)
                a = base + whole
                by_part = [
                    classify([fields_ref[f, k, at, v * LANES : (v + 1) * LANES] for f in range(nf)])
                    for v in range(nv)
                ]
                sheared = []
                for q in range(4):
                    parts = [by_part[v][q] for v in range(nv)]
                    held = halo[k // per][q]
                    to = (LANES - (k % per + 1) * pitch) % LANES
                    held = pltpu.roll(held, to, 1) if to else held
                    own = parts[-1]
                    parts[-1] = jnp.where(lane >= LANES - a, held, own)
                    if frac > 0:
                        far = parts[:-1] + [jnp.where(lane >= LANES - 1 - a, held, own)]
                        far = turn(far, 1, lane)
                        parts = [p + frac * (r - p) for p, r in zip(parts, far)]
                    sheared.append(parts)
                for q in range(3):
                    color[q] = [c + t * s for c, t, s in zip(color[q], clear, sheared[q])]
                clear = [t - t * s for t, s in zip(clear, sheared[3])]
            end = base + 3 * (slices - 1) // 8
            row = row0 + g * SUB + sub
            keep = (row >= low) & (row < high)
            for q in range(4):
                parts = color[q] if q < 3 else [1.0 - t for t in clear]
                parts = turn(parts, end, lane)
                for v in range(nv):
                    out_ref[0, q, 0, at, v * LANES : (v + 1) * LANES] = encode(jnp.where(keep, parts[v], 0.0))
            return carry

        lax.fori_loop(0, rows // SUB, group, 0)


def volume(fields, halo, packed, breakpoints, tf_color, tf_opacity, live, pitch, count_x, count_z, chunk, chunks):
    nf, slices, height, width = fields.shape
    assert slices % 8 == 0
    owned = height // (count_x * count_z)
    part_x = count_x // chunks
    steps = part_x * count_z
    cells = slices * height // chunks * width
    smem = pl.BlockSpec(memory_space=pltpu.SMEM)
    return pl.pallas_call(
        functools.partial(volume_kernel, pitch, chunk * steps),
        grid=(steps,),
        in_specs=[
            smem,
            smem,
            smem,
            smem,
            pl.BlockSpec((nf, slices, owned, width), lambda r: (0, 0, r + chunk * steps, 0)),
            pl.BlockSpec((nf, owned, halo.shape[2]), lambda r: (0, r, 0)),
            *[pl.BlockSpec(memory_space=pl.ANY) for _ in packed],
        ],
        out_specs=pl.BlockSpec((1, 4, 1, owned, width), lambda r: (r % count_z, 0, r // count_z, 0, 0)),
        out_shape=jax.ShapeDtypeStruct((count_z, 4, part_x, owned, width), jnp.int16),
        scratch_shapes=[pltpu.VMEM((8, 8, LANES), jnp.float32)],
        cost_estimate=pl.CostEstimate(flops=cells * 100, bytes_accessed=cells * 40, transcendentals=cells * 2),
        name="volume",
    )(breakpoints, tf_color, tf_opacity, live, fields, halo, *packed)


def merge_kernel(order_ref, src_ref, dst_ref):
    depth = src_ref.shape[0]
    column = lax.axis_index("bx")
    rows = src_ref.shape[3]
    for g in range(0, rows, SUB):
        at = slice(g, g + SUB)
        total = None
        for k in range(depth):
            d = order_ref[column * depth + k]
            part = [decode(src_ref[d, q, 0, at]) for q in range(4)]
            if total is None:
                total = part
            else:
                clear = 1.0 - total[3]
                total = [t + clear * p for t, p in zip(total, part)]
        for q in range(4):
            dst_ref[0, q, at] = encode(total[q])


def merge(arrived, order):
    depth, _, count_x, owned, width = arrived.shape
    return pl.pallas_call(
        merge_kernel,
        grid=(count_x,),
        in_specs=[
            pl.BlockSpec(memory_space=pltpu.SMEM),
            pl.BlockSpec((depth, 4, 1, owned, width), lambda i: (0, 0, i, 0, 0)),
        ],
        out_specs=pl.BlockSpec((1, 4, owned, width), lambda i: (i, 0, 0, 0)),
        out_shape=jax.ShapeDtypeStruct((count_x, 4, owned, width), jnp.int16),
        name="merge",
    )(order.reshape(-1), arrived)


def open_kernel(src_ref, dst_ref):
    dst_ref[...] = decode(src_ref[0])


def open_image(moved):
    count_x, _, owned, width = moved.shape
    return pl.pallas_call(
        open_kernel,
        grid=(count_x,),
        in_specs=[pl.BlockSpec((1, 4, owned, width), lambda i: (i, 0, 0, 0))],
        out_specs=pl.BlockSpec((4, owned, width), lambda i: (0, 0, i)),
        out_shape=jax.ShapeDtypeStruct((4, owned, count_x * width), jnp.float32),
        name="open_image",
    )(moved)


def per_device(fields, breakpoints, tf_color, tf_opacity, depth_order, live_rows):
    slices = fields.shape[1]
    count_x = lax.axis_size("bx")
    count_z = lax.axis_size("bz")
    reach = 3 * (slices * count_z - 1) // 8 + 1
    pitch = halo_pitch(reach)
    chunks = math.gcd(CHUNKS, count_x)
    live = live_rows.reshape(2)
    colors = tf_color.reshape(-1)
    route = [(i, i + 1) for i in range(count_x - 1)]
    rims = [pack_halo(fields, pitch, c, chunks) for c in range(chunks)]
    halos = []
    for c in range(chunks):
        halos.append(lax.ppermute(rims[c], "bx", route))
    merged = []
    for c in range(chunks):
        partial = volume(
            fields, halos[c], rims, breakpoints, colors, tf_opacity, live, pitch, count_x, count_z, c, chunks
        )
        arrived = lax.all_to_all(partial, "bz", split_axis=0, concat_axis=0, tiled=True)
        merged.append(merge(arrived, depth_order))
    merged = jnp.concatenate(merged, axis=0)
    moved = lax.all_to_all(merged, "bx", split_axis=0, concat_axis=0, tiled=True)
    return open_image(moved)


def solution(mesh):
    return jax.shard_map(
        per_device,
        mesh=mesh,
        in_specs=(P(None, "bz", None, "bx"), P(), P(), P(), P(), P("bx", "bz", None)),
        out_specs=P(None, ("bx", "bz"), None),
        check_vma=False,
    )
```

```python
import functools
import math

import jax
import jax.numpy as jnp
from jax import lax
from jax.experimental import pallas as pl
from jax.experimental.pallas import tpu as pltpu
from jax.sharding import PartitionSpec as P


LANES = 128
SUB = 16
LOG2E = 1.4426950408889634
CODE = 65535.0
CHUNKS = 2


def encode(value):
    root = jnp.sqrt(jnp.sqrt(jnp.maximum(value, 0.0)))
    return jnp.round(root * CODE - 32768.0).astype(jnp.int32).astype(jnp.int16)


def decode(code):
    root = (code.astype(jnp.int32).astype(jnp.float32) + 32768.0) * (1.0 / CODE)
    square = root * root
    return square * square


def halo_pitch(reach):
    pitch = 16
    while pitch < reach:
        pitch *= 2
    return pitch


def pack_kernel(pitch, src_ref, dst_ref):
    slices = src_ref.shape[1]
    per = LANES // pitch
    lane = lax.broadcasted_iota(jnp.int32, (src_ref.shape[2], LANES), 1)
    for f in range(src_ref.shape[0]):
        for v in range(dst_ref.shape[2] // LANES):
            total = jnp.zeros((src_ref.shape[2], LANES), jnp.float32)
            for s in range(per):
                k = v * per + s
                if k < slices:
                    x = src_ref[f, k].astype(jnp.float32)
                    x = pltpu.roll(x, (s + 1) * pitch % LANES, 1)
                    slot = (lane >= s * pitch) & (lane < (s + 1) * pitch)
                    total = jnp.where(slot, x, total)
            dst_ref[f, :, v * LANES : (v + 1) * LANES] = total.astype(jnp.bfloat16)


def pack_halo(fields, pitch, chunk, chunks):
    nf, slices, height, width = fields.shape
    rows = math.gcd(256, height // chunks)
    lanes = -(-slices * pitch // LANES) * LANES
    steps = height // chunks // rows
    return pl.pallas_call(
        functools.partial(pack_kernel, pitch),
        grid=(steps,),
        in_specs=[
            pl.BlockSpec((nf, slices, rows, LANES), lambda r: (0, 0, r + chunk * steps, width // LANES - 1))
        ],
        out_specs=pl.BlockSpec((nf, rows, lanes), lambda r: (0, r, 0)),
        out_shape=jax.ShapeDtypeStruct((nf, height // chunks, lanes), jnp.bfloat16),
        cost_estimate=pl.CostEstimate(
            flops=height // chunks * LANES * nf * slices * 4,
            bytes_accessed=height // chunks * LANES * nf * slices * 2,
            transcendentals=0,
        ),
        name="pack_halo",
    )(fields)


def build_tables(marks_ref, color_ref, opacity_ref, tab_ref):
    nbp = marks_ref.shape[0]
    lane = lax.broadcasted_iota(jnp.int32, (8, LANES), 0)

    def spread(value):
        total = jnp.zeros((8, LANES), jnp.float32)
        for j in range(nbp - 1):
            total = jnp.where(lane == j, value(j), total)
        return total

    mark = lambda j: marks_ref[j].astype(jnp.float32)
    start = spread(mark)
    step = jnp.where(lane < nbp - 1, spread(lambda j: mark(j + 1)) - start, 1.0)
    for q in range(4):
        value = (lambda j: color_ref[3 * j + q]) if q < 3 else (lambda j: opacity_ref[j])
        first = spread(value)
        slope = (spread(lambda j: value(j + 1)) - first) / step
        base = first - slope * start
        scale = 1.0 if q < 3 else -LOG2E
        tab_ref[2 * q] = base * scale
        tab_ref[2 * q + 1] = slope * scale


def make_classify(marks_ref, tab_ref):
    nbp = marks_ref.shape[0]
    marks = [marks_ref[j].astype(jnp.float32) for j in range(nbp)]
    rows_of = lambda q: tab_ref[q]

    def look(q, seg):
        return jnp.concatenate([jnp.take_along_axis(rows_of(q), seg[i : i + 8], axis=0, mode="promise_in_bounds") for i in range(0, SUB, 8)], axis=0)

    def classify(raw):
        x0, x1, x2, x3 = [r.astype(jnp.float32) for r in raw]
        level = 127.5 * jnp.tanh(0.5 * x0) + 127.5
        swirl = x1 * x1 + x2 * x2 + x3 * x3
        seg = jnp.zeros(level.shape, jnp.int32)
        for j in range(1, nbp - 1):
            seg = jnp.where(level >= marks[j], j, seg)
        rate = look(6, seg) + look(7, seg) * level
        alpha = 1.0 - jnp.exp2(rate * (0.25 + swirl))
        return [alpha * (look(2 * q, seg) + look(2 * q + 1, seg) * level) for q in range(3)] + [alpha]

    return classify


def turn(parts, shift, lane):
    rolled = [pltpu.roll(p, shift, 1) for p in parts]
    return [jnp.where(lane < shift, rolled[i - 1], rolled[i]) for i in range(len(parts))]


def turn_back(parts, lane):
    rolled = [pltpu.roll(p, LANES - 1, 1) for p in parts]
    n = len(parts)
    return [jnp.where(lane == LANES - 1, rolled[(i + 1) % n], rolled[i]) for i in range(n)]


def volume_kernel(pitch, first_step, marks_ref, color_ref, opacity_ref, live_ref, fields_ref, halo_ref, *rest):
    out_ref, tab_ref = rest[-2:]
    nf, slices, rows, width = fields_ref.shape
    nv = width // LANES
    per = LANES // pitch
    step = pl.program_id(0)

    @pl.when(step == 0)
    def _():
        build_tables(marks_ref, color_ref, opacity_ref, tab_ref)

    low = live_ref[0]
    high = live_ref[1]
    row0 = (step + first_step) * rows
    alive = (row0 < high) & (row0 + rows > low)
    edge = jnp.where(lax.axis_index("bx") > 0, 1.0, 0.0).astype(jnp.float32)
    base = 3 * (lax.axis_index("bz") * slices) // 8

    @pl.when(jnp.logical_not(alive))
    def _():
        out_ref[...] = jnp.full(out_ref.shape, -32768, jnp.int16)

    @pl.when(alive)
    def _():
        lane = lax.broadcasted_iota(jnp.int32, (SUB, LANES), 1)
        sub = lax.broadcasted_iota(jnp.int32, (SUB, LANES), 0)
        classify = make_classify(marks_ref, tab_ref)

        def group(g, carry):
            at = pl.ds(pl.multiple_of(g * SUB, SUB), SUB)
            halo = []
            for v in range(halo_ref.shape[2] // LANES):
                s = classify([halo_ref[f, at, v * LANES : (v + 1) * LANES] for f in range(nf)])
                halo.append([c * edge for c in s])
            color = [[jnp.zeros((SUB, LANES), jnp.float32) for _ in range(nv)] for _ in range(3)]
            clear = [jnp.ones((SUB, LANES), jnp.float32) for _ in range(nv)]
            for k in range(slices):
                whole = 3 * k // 8
                frac = (3 * k % 8) / 8.0
                if k > 0 and whole > 3 * (k - 1) // 8:
                    color = [turn_back(c, lane) for c in color]
                    clear = turn_back(clear, lane)
                a = base + whole
                by_part = [
                    classify([fields_ref[f, k, at, v * LANES : (v + 1) * LANES] for f in range(nf)])
                    for v in range(nv)
                ]
                sheared = []
                for q in range(4):
                    parts = [by_part[v][q] for v in range(nv)]
                    held = halo[k // per][q]
                    to = (LANES - (k % per + 1) * pitch) % LANES
                    held = pltpu.roll(held, to, 1) if to else held
                    own = parts[-1]
                    parts[-1] = jnp.where(lane >= LANES - a, held, own)
                    if frac > 0:
                        far = parts[:-1] + [jnp.where(lane >= LANES - 1 - a, held, own)]
                        far = turn(far, 1, lane)
                        parts = [p + frac * (r - p) for p, r in zip(parts, far)]
                    sheared.append(parts)
                for q in range(3):
                    color[q] = [c + t * s for c, t, s in zip(color[q], clear, sheared[q])]
                clear = [t - t * s for t, s in zip(clear, sheared[3])]
            end = base + 3 * (slices - 1) // 8
            row = row0 + g * SUB + sub
            keep = (row >= low) & (row < high)
            for q in range(4):
                parts = color[q] if q < 3 else [1.0 - t for t in clear]
                parts = turn(parts, end, lane)
                for v in range(nv):
                    out_ref[0, q, 0, at, v * LANES : (v + 1) * LANES] = encode(jnp.where(keep, parts[v], 0.0))
            return carry

        lax.fori_loop(0, rows // SUB, group, 0)


def volume(fields, halo, packed, breakpoints, tf_color, tf_opacity, live, pitch, count_x, count_z, chunk, chunks):
    nf, slices, height, width = fields.shape
    assert slices % 8 == 0
    owned = height // (count_x * count_z)
    part_x = count_x // chunks
    steps = part_x * count_z
    cells = slices * height // chunks * width
    smem = pl.BlockSpec(memory_space=pltpu.SMEM)
    return pl.pallas_call(
        functools.partial(volume_kernel, pitch, chunk * steps),
        grid=(steps,),
        in_specs=[
            smem,
            smem,
            smem,
            smem,
            pl.BlockSpec((nf, slices, owned, width), lambda r: (0, 0, r + chunk * steps, 0)),
            pl.BlockSpec((nf, owned, halo.shape[2]), lambda r: (0, r, 0)),
            *[pl.BlockSpec(memory_space=pl.ANY) for _ in packed],
        ],
        out_specs=pl.BlockSpec((1, 4, 1, owned, width), lambda r: (r % count_z, 0, r // count_z, 0, 0)),
        out_shape=jax.ShapeDtypeStruct((count_z, 4, part_x, owned, width), jnp.int16),
        scratch_shapes=[pltpu.VMEM((8, 8, LANES), jnp.float32)],
        cost_estimate=pl.CostEstimate(flops=cells * 100, bytes_accessed=cells * 40, transcendentals=cells * 2),
        name="volume",
    )(breakpoints, tf_color, tf_opacity, live, fields, halo, *packed)


def merge_kernel(order_ref, src_ref, dst_ref):
    depth = src_ref.shape[0]
    column = lax.axis_index("bx")
    rows = src_ref.shape[3]
    for i in range(dst_ref.shape[0]):
        for g in range(0, rows, SUB):
            at = slice(g, g + SUB)
            total = None
            for k in range(depth):
                d = order_ref[column * depth + k]
                part = [decode(src_ref[d, q, i, at]) for q in range(4)]
                if total is None:
                    total = part
                else:
                    clear = 1.0 - total[3]
                    total = [t + clear * p for t, p in zip(total, part)]
            for q in range(4):
                dst_ref[i, q, at] = encode(total[q])


def merge(arrived, order):
    depth, _, count_x, owned, width = arrived.shape
    many = math.gcd(2, count_x)
    return pl.pallas_call(
        merge_kernel,
        grid=(count_x // many,),
        in_specs=[
            pl.BlockSpec(memory_space=pltpu.SMEM),
            pl.BlockSpec((depth, 4, many, owned, width), lambda i: (0, 0, i, 0, 0)),
        ],
        out_specs=pl.BlockSpec((many, 4, owned, width), lambda i: (i, 0, 0, 0)),
        out_shape=jax.ShapeDtypeStruct((count_x, 4, owned, width), jnp.int16),
        name="merge",
    )(order.reshape(-1), arrived)


def open_kernel(src_ref, dst_ref):
    width = src_ref.shape[3]
    for i in range(src_ref.shape[0]):
        dst_ref[:, :, i * width : (i + 1) * width] = decode(src_ref[i])


def open_image(moved):
    count_x, _, owned, width = moved.shape
    many = math.gcd(4, count_x)
    return pl.pallas_call(
        open_kernel,
        grid=(count_x // many,),
        in_specs=[pl.BlockSpec((many, 4, owned, width), lambda i: (i, 0, 0, 0))],
        out_specs=pl.BlockSpec((4, owned, many * width), lambda i: (0, 0, i)),
        out_shape=jax.ShapeDtypeStruct((4, owned, count_x * width), jnp.float32),
        name="open_image",
    )(moved)


def per_device(fields, breakpoints, tf_color, tf_opacity, depth_order, live_rows):
    slices = fields.shape[1]
    count_x = lax.axis_size("bx")
    count_z = lax.axis_size("bz")
    reach = 3 * (slices * count_z - 1) // 8 + 1
    pitch = halo_pitch(reach)
    chunks = math.gcd(CHUNKS, count_x)
    live = live_rows.reshape(2)
    colors = tf_color.reshape(-1)
    route = [(i, i + 1) for i in range(count_x - 1)]
    rims = [pack_halo(fields, pitch, c, chunks) for c in range(chunks)]
    halos = []
    for c in range(chunks):
        halos.append(lax.ppermute(rims[c], "bx", route))
    merged = []
    for c in range(chunks):
        partial = volume(
            fields, halos[c], rims, breakpoints, colors, tf_opacity, live, pitch, count_x, count_z, c, chunks
        )
        arrived = lax.all_to_all(partial, "bz", split_axis=0, concat_axis=0, tiled=True)
        merged.append(merge(arrived, depth_order))
    merged = jnp.concatenate(merged, axis=0)
    moved = lax.all_to_all(merged, "bx", split_axis=0, concat_axis=0, tiled=True)
    return open_image(moved)


def solution(mesh):
    return jax.shard_map(
        per_device,
        mesh=mesh,
        in_specs=(P(None, "bz", None, "bx"), P(), P(), P(), P(), P("bx", "bz", None)),
        out_specs=P(None, ("bx", "bz"), None),
        check_vma=False,
    )
```
